32 devices in a mesh: ctx: 4 (over z), exp: 8 (over y, x, core).
Axes of the slice: x: 2, y: 2, z: 4, core: 2. Of those that a mesh axis runs over, the one named last changes fastest.
Arguments:
- hidden_in: bfloat16 [4096, 2880], P(('ctx', 'exp')), may hold values from -6 to 6
- query_rows: bfloat16 [4096, 2048], P(('ctx', 'exp')), may hold values from -6 to 6
- key_rows: bfloat16 [4096, 256], P(('ctx', 'exp')), may hold values from -6 to 6
- value_rows: bfloat16 [4096, 256], P(('ctx', 'exp')), may hold values from -6 to 6
- sink_logits: float32 [32], replicated, may hold values from -1 to 3
- out_weight: bfloat16 [2048, 2880], replicated, may hold values from -0.125 to 0.125
- norm_gain: float32 [2880], replicated, may hold values from 0.5 to 2
- gate_weight: bfloat16 [32, 2880, 720], P(('ctx', 'exp')), may hold values from -0.109375 to 0.109375
- up_weight: bfloat16 [32, 2880, 720], P(('ctx', 'exp')), may hold values from -0.109375 to 0.109375
- down_weight: bfloat16 [32, 720, 2880], P(('ctx', 'exp')), may hold values from -0.15625 to 0.15625
- expert_ids: int32 [4096, 4], P(('ctx', 'exp')), may hold values from 0 to 15, all different within a row; in each aligned block of 128 rows (0 to 127, 128 to 255, ...) at most 64 rows name the same one
- gate_values: float32 [4096, 4], P(('ctx', 'exp')), may hold values from 0.05 to 0.6
Outputs:
- layer_out: bfloat16 [4096, 2880], P(('ctx', 'exp'))
The draws below stay inside these ranges and needn't reach their ends.
Inputs may be any that keep to these rules, and one draw needn't show every extreme that they name: `expert_ids`: each row names 4 different experts; among the 128 rows of one device no expert is named more than 64 times.
All inputs are finite; a program needn't handle non-finite values.
Results may differ from the reference program's by a relative error of at most 0.0062.
Values may be sent and summed in bfloat16 or wider, within the bound.
A program may use at most 128 MiB of HBM per device.

```python
import math
import jax
import jax.numpy as jnp
import numpy as np
from jax import lax

D = 2880
HEAD_DIM = 64
TOP = 4
HEADS = 32
KV_HEADS = 4
WINDOW = 128
FF = 1440
TOK_DEV = 128
FF_HALF = 720
TOKENS = 4096
EXPERTS = 16
CAP = 64
N_CTX = 4
N_EXP = 8


def draw_query_rows(key, part):
    base_draw = jnp.clip(jax.random.normal(jax.random.fold_in(key, 11), (TOKENS, HEADS * HEAD_DIM), jnp.float32), -4.0, 4.0)
    return base_draw.astype(jnp.bfloat16)


def draw_key_rows(key, part):
    base_draw = jnp.clip(jax.random.normal(jax.random.fold_in(key, 12), (TOKENS, KV_HEADS * HEAD_DIM), jnp.float32), -4.0, 4.0)
    return base_draw.astype(jnp.bfloat16)


def level_of(key, extent, shards, least, high):
    def one(axis_at, blocks):
        draws = jax.random.uniform(jax.random.fold_in(jax.random.fold_in(key, 6), axis_at), (blocks,), jnp.float32, least / len(shards), high / len(shards))
        return jnp.repeat(jnp.exp(draws), extent[axis_at] // blocks).reshape((-1,) + (1,) * (len(extent) - axis_at - 1))

    loudness = one(*shards[0])
    for cut in shards[1:]:
        loudness = loudness * one(*cut)
    return loudness


def shared_out(stream_key, own, number, rows, amount, top, limit, slope):
    ranking = jax.random.permutation(stream_key, amount)
    heavy_load, ordinary = shares(amount, rows * top, limit, slope, True), shares(amount, rows * top, limit, slope, False)
    places = jnp.arange(amount)

    def named(sizes, turn):
        used = int((sizes > 0).sum())
        fixed = max(1, used // 4)
        shifted = fixed + (places - fixed + turn * (used - fixed)) % max(1, amount - fixed)
        return jnp.zeros((amount,), jnp.int32).at[ranking[jnp.where(places < fixed, places, shifted)]].set(jnp.asarray(sizes, jnp.int32))

    sizes = jnp.where(number % 4 == 0, named(heavy_load, number // 4), named(ordinary, number - number // 4 - 1))
    mixed = jax.random.permutation(jax.random.fold_in(own, 3), amount)
    source_of, taker = mixed[0:amount // 2 * 2:2], mixed[1:amount // 2 * 2:2]
    room = jnp.minimum(sizes[source_of] - 1, limit - sizes[taker]) // 2
    room = jnp.where((source_of == ranking[0]) | (taker == ranking[0]) | (sizes[taker] == 0), 0, jnp.maximum(room, 0))
    shifted = jax.random.randint(jax.random.fold_in(own, 4), (amount // 2,), 0, 1 << 20) % (room + 1)
    sizes = sizes.at[source_of].add(-shifted).at[taker].add(shifted)
    members = jnp.searchsorted(jnp.cumsum(sizes), jnp.arange(rows * top), side="right").astype(jnp.int32)
    listing = members.reshape(top, rows).T
    listing = listing[jax.random.permutation(jax.random.fold_in(own, 1), rows)]
    turn = jax.random.randint(jax.random.fold_in(own, 2), (rows, 1), 0, top)
    return jnp.take_along_axis(listing, (jnp.arange(top)[None, :] + turn) % top, axis=1)


def shares(amount, total, reach, slope, full):
    weights = [(1 << 20) // math.isqrt(rank ** slope) + 1 for rank in range(1, amount + 1)]
    largest = reach if full else min(reach, max(-(-total // amount), total * weights[0] // sum(weights)))
    least = 1 if total - largest >= amount - 1 else 0
    given, spare = [largest] + [least] * (amount - 1), total - largest - least * (amount - 1)
    while spare > 0:
        free = [i for i in range(1, amount) if given[i] < largest] or [i for i in range(1, amount) if given[i] < reach]
        pool, remaining = sum([weights[i] for i in free]), spare
        for i in free:
            more = min(reach - given[i], max(1, remaining * weights[i] // pool), spare)
            given[i] = given[i] + more
            spare = spare - more
    return np.array(given)


def gaussian(stream_key, extent, scale, reach, cuts=(), held_as=jnp.bfloat16):
    entries = scale * jax.random.normal(stream_key, extent, jnp.float32)
    if cuts:
        entries = entries * level_of(stream_key, extent, cuts, -0.22, 0.18)
    return jnp.clip(entries, -reach, reach).astype(held_as)


def setup_inputs(seed: int = 0) -> dict:
    seeds = jax.random.split(jax.random.key(seed), 13)
    hidden_in = gaussian(seeds[0], (TOKENS, D), 1.0, 6.0, ((0, 32),))
    query_rows = draw_query_rows(jax.random.fold_in(seeds[12], 71), 0)
    key_rows = draw_key_rows(jax.random.fold_in(seeds[12], 71), 0)
    value_rows = gaussian(seeds[3], (TOKENS, KV_HEADS * HEAD_DIM), 1.0, 6.0, ((0, 32),))
    sink_logits = jnp.clip(jax.random.uniform(seeds[4], (HEADS,), jnp.float32, -1.0, 3.0), -1.0, 3.0)
    out_weight = gaussian(seeds[5], (HEADS * HEAD_DIM, D), (HEADS * HEAD_DIM) ** -0.5, 0.125)
    norm_gain = jnp.clip(jnp.exp(jax.random.uniform(seeds[6], (D,), jnp.float32, math.log(0.5), math.log(2.0))), 0.5, 2.0)
    gate_weight = gaussian(seeds[7], (2 * EXPERTS, D, FF_HALF), D ** -0.5, 0.109375, ((0, 32),))
    up_weight = gaussian(seeds[8], (2 * EXPERTS, D, FF_HALF), D ** -0.5, 0.109375, ((0, 32),))
    down_weight = gaussian(seeds[9], (2 * EXPERTS, FF_HALF, D), FF ** -0.5, 0.15625, ((0, 32),))
    expert_ids_keys = jax.random.split(jax.random.fold_in(seeds[10], 1), TOKENS // TOK_DEV)
    expert_ids_turns = jax.random.permutation(jax.random.fold_in(seeds[10], 3), TOKENS // TOK_DEV)
    expert_ids = jax.vmap(lambda own, number: shared_out(jax.random.fold_in(seeds[10], 2), own, number, TOK_DEV, EXPERTS, TOP, CAP, 2))(expert_ids_keys, expert_ids_turns).reshape((TOKENS, TOP))
    gate_values = jnp.clip(0.05 + 0.55 * jax.random.uniform(seeds[11], (TOKENS, TOP), jnp.float32) ** level_of(seeds[11], (TOKENS, TOP), ((0, 32),), -0.2, 0.2), 0.05, 0.6)
    return dict(hidden_in=hidden_in, query_rows=query_rows, key_rows=key_rows, value_rows=value_rows, sink_logits=sink_logits, out_weight=out_weight, norm_gain=norm_gain, gate_weight=gate_weight, up_weight=up_weight, down_weight=down_weight, expert_ids=expert_ids, gate_values=gate_values)


block_order = 64
norm_eps = 1e-05
masked_score = -1e+30

def hadamard_table():
    indices = jnp.arange(block_order, dtype=jnp.int32)
    parity = jnp.zeros((block_order, block_order), jnp.int32)
    for bit_level in range(6):
        stride = 2 ** bit_level
        parity = parity + indices[:, None] // stride % 2 * (indices[None, :] // stride % 2)
    return (1.0 - 2.0 * (parity % 2)).astype(jnp.float32) / 8.0

def rotate_rows(normed):
    row_count, feature_count = normed.shape
    blocks = normed.reshape(row_count, feature_count // block_order, block_order)
    turned = jnp.einsum('tbi,ij->tbj', blocks, hadamard_table(), precision=lax.Precision.HIGHEST)
    return turned.reshape(row_count, feature_count).astype(jnp.bfloat16)

def expert_half(row_block, gate_part, up_part, down_part):
    gate_val = jnp.dot(row_block, gate_part, preferred_element_type=jnp.float32)
    up_val = jnp.dot(row_block, up_part, preferred_element_type=jnp.float32)
    active = (gate_val * jax.nn.sigmoid(1.702 * gate_val) * (up_val + 1.0)).astype(jnp.bfloat16)
    return jnp.dot(active, down_part, preferred_element_type=jnp.float32).astype(jnp.bfloat16)

def attend(query_block, key_block, value_block, sink_logits, query_pos, key_pos):
    scores = jnp.einsum('tkgd,skd->kgts', query_block.astype(jnp.float32), key_block.astype(jnp.float32))
    scores = scores * HEAD_DIM ** (-0.5)
    allowed = (key_pos[None, :] <= query_pos[:, None]) & (key_pos[None, :] > query_pos[:, None] - WINDOW) & (key_pos[None, :] >= 0)
    scores = jnp.where(allowed[None, None], scores, masked_score)
    sink_col = sink_logits.astype(jnp.float32).reshape(scores.shape[0], scores.shape[1])[:, :, None]
    largest = jnp.maximum(lax.optimization_barrier(jnp.max(scores, axis=-1)), sink_col)
    weights = jnp.exp(scores - largest[..., None])
    denom_sum = lax.optimization_barrier(jnp.sum(weights, axis=-1)) + jnp.exp(sink_col - largest)
    prob_bf = (weights / denom_sum[..., None]).astype(jnp.bfloat16)
    mixed_out = jnp.einsum('kgts,skd->tkgd', prob_bf.astype(jnp.float32), value_block.astype(jnp.float32))
    return mixed_out.astype(jnp.bfloat16)

def attention_all(query_rows, key_rows, value_rows, sink_logits):
    total_rows = query_rows.shape[0]
    kv_count = key_rows.shape[1] // HEAD_DIM
    group_size = query_rows.shape[1] // HEAD_DIM // kv_count
    padded_keys = jnp.concatenate([jnp.zeros((WINDOW, key_rows.shape[1]), key_rows.dtype), key_rows], axis=0)
    padded_values = jnp.concatenate([jnp.zeros((WINDOW, value_rows.shape[1]), value_rows.dtype), value_rows], axis=0)

    def one_block(block_index):
        start_row = (block_index * WINDOW).astype(jnp.int32)
        query_block = lax.dynamic_slice_in_dim(query_rows, start_row, WINDOW, 0).reshape(WINDOW, kv_count, group_size, HEAD_DIM)
        key_block = lax.dynamic_slice_in_dim(padded_keys, start_row, 2 * WINDOW, 0).reshape(2 * WINDOW, kv_count, HEAD_DIM)
        value_block = lax.dynamic_slice_in_dim(padded_values, start_row, 2 * WINDOW, 0).reshape(2 * WINDOW, kv_count, HEAD_DIM)
        query_pos = start_row + jnp.arange(WINDOW, dtype=jnp.int32)
        key_pos = start_row - WINDOW + jnp.arange(2 * WINDOW, dtype=jnp.int32)
        return attend(query_block, key_block, value_block, sink_logits, query_pos, key_pos).reshape(WINDOW, -1)
    blocks = lax.map(one_block, jnp.arange(total_rows // WINDOW, dtype=jnp.int32))
    return blocks.reshape(total_rows, -1)

def reference(hidden_in, query_rows, key_rows, value_rows, sink_logits, out_weight, norm_gain, gate_weight, up_weight, down_weight, expert_ids, gate_values):
    attended = attention_all(query_rows, key_rows, value_rows, sink_logits)
    mid_stream = hidden_in.astype(jnp.float32) + jnp.dot(attended, out_weight, preferred_element_type=jnp.float32)
    normed = mid_stream * lax.rsqrt(lax.optimization_barrier(jnp.mean(mid_stream * mid_stream, axis=-1, keepdims=True)) + norm_eps) * norm_gain.astype(jnp.float32)
    rotated = rotate_rows(normed)
    top_count = expert_ids.shape[1]
    flat_ids = expert_ids.reshape(-1).astype(jnp.int32)
    expert_total = gate_weight.shape[0] // 2
    sort_order = jnp.argsort(flat_ids, stable=True).astype(jnp.int32)
    counts = lax.optimization_barrier(jnp.sum((flat_ids[:, None] == jnp.arange(expert_total, dtype=jnp.int32)[None, :]).astype(jnp.int32), axis=0))
    offsets = (jnp.cumsum(counts) - counts).astype(jnp.int32)
    slot_bound = N_CTX * N_EXP * CAP
    token_sorted = jnp.concatenate([sort_order // top_count, jnp.zeros((slot_bound,), jnp.int32)]).astype(jnp.int32)
    weight_sorted = jnp.concatenate([gate_values.reshape(-1)[sort_order].astype(jnp.float32), jnp.zeros((slot_bound,), jnp.float32)])

    def add_expert(accum, expert):
        start_row = offsets[expert]
        tokens_here = lax.dynamic_slice_in_dim(token_sorted, start_row, slot_bound, 0)
        weights_here = lax.dynamic_slice_in_dim(weight_sorted, start_row, slot_bound, 0)
        is_valid = jnp.arange(slot_bound, dtype=jnp.int32) < counts[expert]
        row_block = rotated[tokens_here]
        first_half = expert_half(row_block, gate_weight[2 * expert], up_weight[2 * expert], down_weight[2 * expert])
        second = expert_half(row_block, gate_weight[2 * expert + 1], up_weight[2 * expert + 1], down_weight[2 * expert + 1])
        scaled = jnp.where(is_valid, weights_here, jnp.zeros_like(weights_here))
        contrib = (first_half.astype(jnp.float32) + second.astype(jnp.float32)) * scaled[:, None]
        return (accum.at[tokens_here].add(contrib), None)
    expert_sum, unused = lax.scan(add_expert, jnp.zeros(mid_stream.shape, jnp.float32), jnp.arange(expert_total, dtype=jnp.int32))
    return (mid_stream + expert_sum).astype(jnp.bfloat16)
```

```python
import jax
import jax.numpy as jnp
from jax import lax
from jax.experimental import pallas as pl
from jax.experimental.pallas import tpu as pltpu
from jax.sharding import Mesh, PartitionSpec as P

HEAD_DIM = 64
WINDOW = 128


AXES = ("ctx", "chip", "core")
CHIPS = ("ctx", "chip")

block_order = 64
norm_eps = 1e-05
masked_score = -1e30


def passed_along(value, axis, by):
    length = lax.axis_size(axis)
    pairs = [(i, i + by) for i in range(length) if 0 <= i + by < length]
    return lax.ppermute(value, axis, pairs)


def hadamard_table():
    indices = jnp.arange(block_order, dtype=jnp.int32)
    parity = jnp.zeros((block_order, block_order), jnp.int32)
    for bit_level in range(6):
        stride = 2**bit_level
        parity = parity + indices[:, None] // stride % 2 * (indices[None, :] // stride % 2)
    return (1.0 - 2.0 * (parity % 2)).astype(jnp.float32) / 8.0


def rotate_rows(normed):
    row_count, feature_count = normed.shape
    blocks = normed.reshape(row_count, feature_count // block_order, block_order)
    turned = jnp.einsum("tbi,ij->tbj", blocks, hadamard_table(), precision=lax.Precision.HIGHEST)
    return turned.reshape(row_count, feature_count).astype(jnp.bfloat16)


def ffn_body(row_ref, gate_ref, up_ref, down_ref, out_ref):
    rows = row_ref[...]
    gate_val = jnp.dot(rows, gate_ref[0], preferred_element_type=jnp.float32)
    up_val = jnp.dot(rows, up_ref[0], preferred_element_type=jnp.float32)
    active = (gate_val * jax.nn.sigmoid(1.702 * gate_val) * (up_val + 1.0)).astype(jnp.bfloat16)
    out_ref[...] = jnp.dot(active, down_ref[0], preferred_element_type=jnp.float32).astype(
        out_ref.dtype
    )


def expert_half(row_block, gate_part, up_part, down_part):
    row_total, feature_count = row_block.shape
    tile = 256

    def whole(part):
        return pl.BlockSpec(part.shape, lambda i: (0, 0, 0), pipeline_mode=pl.Buffered(1))

    def rows():
        return pl.BlockSpec((tile, feature_count), lambda i: (i, 0))

    weight_count = gate_part.size + up_part.size + down_part.size
    return pl.pallas_call(
        ffn_body,
        out_shape=jax.ShapeDtypeStruct(row_block.shape, jnp.bfloat16),
        grid=(row_total // tile,),
        in_specs=[rows(), whole(gate_part), whole(up_part), whole(down_part)],
        out_specs=rows(),
        compiler_params=pltpu.CompilerParams(vmem_limit_bytes=40 << 20),
        cost_estimate=pl.CostEstimate(
            flops=2 * row_total * weight_count,
            bytes_accessed=2 * weight_count + 4 * row_total * feature_count,
            transcendentals=row_total * gate_part.shape[2],
        ),
    )(row_block, gate_part, up_part, down_part)


def attend(query_block, key_block, value_block, sink_logits, query_pos, key_pos):
    scores = jnp.einsum(
        "tkgd,skd->kgts", query_block, key_block, preferred_element_type=jnp.float32
    )
    scores = scores * HEAD_DIM ** (-0.5)
    allowed = (
        (key_pos[None, :] <= query_pos[:, None])
        & (key_pos[None, :] > query_pos[:, None] - WINDOW)
        & (key_pos[None, :] >= 0)
    )
    scores = jnp.where(allowed[None, None], scores, masked_score)
    sink_col = sink_logits.reshape(scores.shape[0], scores.shape[1])[:, :, None]
    largest = jnp.maximum(jnp.max(scores, axis=-1), sink_col)
    weights = jnp.exp(scores - largest[..., None])
    denom_sum = jnp.sum(weights, axis=-1) + jnp.exp(sink_col - largest)
    prob_bf = (weights / denom_sum[..., None]).astype(jnp.bfloat16)
    mixed_out = jnp.einsum(
        "kgts,skd->tkgd", prob_bf, value_block, preferred_element_type=jnp.float32
    )
    return mixed_out.astype(jnp.bfloat16)


def local(
    hidden_in,
    query_rows,
    key_rows,
    value_rows,
    sink_logits,
    out_weight,
    norm_gain,
    gate_weight,
    up_weight,
    down_weight,
    expert_ids,
    gate_values,
):
    row_count, feature_count = hidden_in.shape
    slot_hot, slot_gate = route_tables(expert_ids, gate_values, lax.axis_size(CHIPS))
    kv_count = key_rows.shape[1] // HEAD_DIM
    head_count = sink_logits.shape[0]
    group_size = head_count // kv_count
    prior_keys, prior_values = passed_along((key_rows, value_rows), AXES, 1)
    all_keys = jnp.concatenate([prior_keys, key_rows], axis=0).reshape(
        WINDOW + row_count, kv_count, HEAD_DIM
    )
    all_values = jnp.concatenate([prior_values, value_rows], axis=0).reshape(
        WINDOW + row_count, kv_count, HEAD_DIM
    )
    anchor = lax.axis_index(AXES) * row_count
    query_pos = anchor + jnp.arange(row_count, dtype=jnp.int32)
    key_pos = anchor - WINDOW + jnp.arange(WINDOW + row_count, dtype=jnp.int32)
    attended = attend(
        query_rows.reshape(row_count, kv_count, group_size, HEAD_DIM),
        all_keys,
        all_values,
        sink_logits,
        query_pos,
        key_pos,
    )
    attended = attended.reshape(row_count, head_count * HEAD_DIM)
    mid_stream = hidden_in.astype(jnp.float32) + jnp.dot(
        attended, out_weight, preferred_element_type=jnp.float32
    )
    normed = (
        mid_stream
        * lax.rsqrt(jnp.mean(mid_stream * mid_stream, axis=-1, keepdims=True) + norm_eps)
        * norm_gain
    )
    rotated = rotate_rows(normed)
    packed = jnp.dot(
        slot_hot.astype(jnp.bfloat16).T, rotated, preferred_element_type=jnp.float32
    ).astype(jnp.bfloat16)
    expert_total = lax.axis_size(CHIPS)
    outgoing = packed.reshape(expert_total, -1, feature_count)
    arrived = lax.all_to_all(outgoing, CHIPS, split_axis=0, concat_axis=0, tiled=True)
    mine = arrived.reshape(-1, feature_count)
    swap = [(0, 1), (1, 0)]
    theirs = lax.ppermute(mine, "core", swap)
    made_mine = expert_half(mine, gate_weight, up_weight, down_weight)
    made_theirs = expert_half(theirs, gate_weight, up_weight, down_weight)
    other_half = lax.ppermute(made_theirs, "core", swap)
    summed = (made_mine.astype(jnp.float32) + other_half.astype(jnp.float32)).astype(jnp.bfloat16)
    returned = lax.all_to_all(
        summed.reshape(arrived.shape), CHIPS, split_axis=0, concat_axis=0, tiled=True
    ).reshape(-1, feature_count)
    gate_high = lax.reduce_precision(slot_gate, 8, 7)
    gate_parts = jnp.concatenate([gate_high, slot_gate - gate_high], axis=0).astype(jnp.bfloat16)
    weighted = jnp.dot(gate_parts, returned, preferred_element_type=jnp.float32)
    expert_sum = weighted[:row_count] + weighted[row_count:]
    return (mid_stream + expert_sum).astype(jnp.bfloat16)


def route_tables(expert_ids, gate_values, expert_total):
    row_count, top_count = expert_ids.shape
    capacity = max(2, 2 * row_count * top_count // expert_total)
    experts = jnp.arange(expert_total, dtype=jnp.int32)
    named = expert_ids[:, :, None] == experts[None, None, :]
    chosen = jnp.any(named, axis=1).astype(jnp.float32)
    row_axis = jnp.arange(row_count, dtype=jnp.int32)
    earlier = (row_axis[:, None] > row_axis[None, :]).astype(jnp.float32)
    rank = jnp.dot(earlier, chosen, preferred_element_type=jnp.float32)
    route_rank = jnp.sum(jnp.where(named, rank[:, None, :], 0.0), axis=2).astype(jnp.int32)
    slot = expert_ids * capacity + route_rank
    slots = jnp.arange(expert_total * capacity, dtype=jnp.int32)
    slot_hot = jnp.zeros((row_count, slots.shape[0]), jnp.float32)
    slot_gate = slot_hot
    for k in range(top_count):
        here = slot[:, k : k + 1] == slots[None, :]
        slot_hot = jnp.where(here, 1.0, slot_hot)
        slot_gate = jnp.where(here, gate_values[:, k : k + 1], slot_gate)
    return slot_hot, slot_gate


def solution(mesh):
    ctx_size, exp_size = mesh.devices.shape
    mesh = Mesh(mesh.devices.reshape(ctx_size, exp_size // 2, 2), AXES)
    in_specs = (
        P(AXES, None),
        P(AXES, None),
        P(AXES, None),
        P(AXES, None),
        P(),
        P(),
        P(),
        P(AXES, None, None),
        P(AXES, None, None),
        P(AXES, None, None),
        P(AXES, None),
        P(AXES, None),
    )
    out_specs = P(AXES, None)
    return jax.shard_map(local, mesh=mesh, in_specs=in_specs, out_specs=out_specs, check_vma=False)
```

```python
import jax
import jax.numpy as jnp
from jax import lax
from jax.experimental import pallas as pl
from jax.experimental.pallas import tpu as pltpu
from jax.sharding import Mesh, PartitionSpec as P

HEAD_DIM = 64
WINDOW = 128


AXES = ("ctx", "chip", "core")
CHIPS = ("ctx", "chip")
CHUNKS = 2

block_order = 64
norm_eps = 1e-05
masked_score = -1e30


def passed_along(value, axis, by):
    length = lax.axis_size(axis)
    pairs = [(i, i + by) for i in range(length) if 0 <= i + by < length]
    return lax.ppermute(value, axis, pairs)


def hadamard_table():
    indices = jnp.arange(block_order, dtype=jnp.int32)
    parity = jnp.zeros((block_order, block_order), jnp.int32)
    for bit_level in range(6):
        stride = 2**bit_level
        parity = parity + indices[:, None] // stride % 2 * (indices[None, :] // stride % 2)
    return (1.0 - 2.0 * (parity % 2)).astype(jnp.float32) / 8.0


def rotate_rows(normed):
    row_count, feature_count = normed.shape
    blocks = normed.reshape(row_count, feature_count // block_order, block_order)
    turned = jnp.einsum("tbi,ij->tbj", blocks, hadamard_table(), precision=lax.Precision.HIGHEST)
    return turned.reshape(row_count, feature_count).astype(jnp.bfloat16)


def contract_last(rows, part):
    return lax.dot_general(
        rows, part, (((1,), (1,)), ((), ())), preferred_element_type=jnp.float32
    )


def ffn_body(mine_ref, theirs_ref, gate_ref, up_ref, down_ref, mine_out, theirs_out):
    for row_ref, out_ref in ((mine_ref, mine_out), (theirs_ref, theirs_out)):
        rows = row_ref[...]
        gate_val = contract_last(rows, gate_ref[0])
        up_val = contract_last(rows, up_ref[0])
        active = gate_val * jax.nn.sigmoid(1.702 * gate_val) * (up_val + 1.0)
        out_ref[...] = jnp.dot(
            active.astype(jnp.bfloat16), down_ref[0], preferred_element_type=jnp.float32
        ).astype(out_ref.dtype)


def expert_half(mine, theirs, gate_part, up_part, down_part):
    row_total, feature_count = mine.shape
    tile = 256

    def whole(part):
        return pl.BlockSpec(part.shape, lambda i: (0, 0, 0), pipeline_mode=pl.Buffered(1))

    def rows():
        return pl.BlockSpec((tile, feature_count), lambda i: (i, 0))

    weight_count = gate_part.size + up_part.size + down_part.size
    return pl.pallas_call(
        ffn_body,
        out_shape=[jax.ShapeDtypeStruct(mine.shape, jnp.bfloat16)] * 2,
        grid=(row_total // tile,),
        in_specs=[rows(), rows(), whole(gate_part), whole(up_part), whole(down_part)],
        out_specs=[rows(), rows()],
        compiler_params=pltpu.CompilerParams(vmem_limit_bytes=48 << 20),
        cost_estimate=pl.CostEstimate(
            flops=4 * row_total * weight_count,
            bytes_accessed=2 * weight_count + 8 * row_total * feature_count,
            transcendentals=2 * row_total * gate_part.shape[1],
        ),
    )(mine, theirs, gate_part, up_part, down_part)


def pack_body(hot_ref, row_ref, out_ref):
    out_ref[...] = jnp.dot(hot_ref[...], row_ref[...], preferred_element_type=jnp.float32).astype(
        out_ref.dtype
    )


def pack_rows(hot, rows):
    slot_total, row_count = hot.shape
    feature_count = rows.shape[1]
    tile = 256
    return pl.pallas_call(
        pack_body,
        out_shape=jax.ShapeDtypeStruct((slot_total, feature_count), jnp.bfloat16),
        grid=(slot_total // tile,),
        in_specs=[
            pl.BlockSpec((tile, row_count), lambda i: (i, 0)),
            pl.BlockSpec((row_count, feature_count), lambda i: (0, 0)),
        ],
        out_specs=pl.BlockSpec((tile, feature_count), lambda i: (i, 0)),
        cost_estimate=pl.CostEstimate(
            flops=2 * slot_total * row_count * feature_count,
            bytes_accessed=2 * slot_total * feature_count,
            transcendentals=0,
        ),
    )(hot, rows)


def attend(query_block, key_block, value_block, sink_logits, query_pos, key_pos):
    scores = jnp.einsum(
        "tkgd,skd->kgts", query_block, key_block, preferred_element_type=jnp.float32
    )
    scores = scores * HEAD_DIM ** (-0.5)
    allowed = (
        (key_pos[None, :] <= query_pos[:, None])
        & (key_pos[None, :] > query_pos[:, None] - WINDOW)
        & (key_pos[None, :] >= 0)
    )
    scores = jnp.where(allowed[None, None], scores, masked_score)
    sink_col = sink_logits.reshape(scores.shape[0], scores.shape[1])[:, :, None]
    largest = jnp.maximum(jnp.max(scores, axis=-1), sink_col)
    weights = jnp.exp(scores - largest[..., None])
    denom_sum = jnp.sum(weights, axis=-1) + jnp.exp(sink_col - largest)
    prob_bf = (weights / denom_sum[..., None]).astype(jnp.bfloat16)
    mixed_out = jnp.einsum(
        "kgts,skd->tkgd", prob_bf, value_block, preferred_element_type=jnp.float32
    )
    return mixed_out.astype(jnp.bfloat16)


def local(
    hidden_in,
    query_rows,
    key_rows,
    value_rows,
    sink_logits,
    out_weight,
    norm_gain,
    gate_weight,
    up_weight,
    down_weight,
    expert_ids,
    gate_values,
):
    row_count, feature_count = hidden_in.shape
    slot_hot, slot_gate = route_tables(expert_ids, gate_values, lax.axis_size(CHIPS))
    kv_count = key_rows.shape[1] // HEAD_DIM
    head_count = sink_logits.shape[0]
    group_size = head_count // kv_count
    prior_keys, prior_values = passed_along((key_rows, value_rows), AXES, 1)
    all_keys = jnp.concatenate([prior_keys, key_rows], axis=0).reshape(
        WINDOW + row_count, kv_count, HEAD_DIM
    )
    all_values = jnp.concatenate([prior_values, value_rows], axis=0).reshape(
        WINDOW + row_count, kv_count, HEAD_DIM
    )
    anchor = lax.axis_index(AXES) * row_count
    query_pos = anchor + jnp.arange(row_count, dtype=jnp.int32)
    key_pos = anchor - WINDOW + jnp.arange(WINDOW + row_count, dtype=jnp.int32)
    attended = attend(
        query_rows.reshape(row_count, kv_count, group_size, HEAD_DIM),
        all_keys,
        all_values,
        sink_logits,
        query_pos,
        key_pos,
    )
    attended = attended.reshape(row_count, head_count * HEAD_DIM)
    mid_stream = hidden_in.astype(jnp.float32) + jnp.dot(
        attended, out_weight, preferred_element_type=jnp.float32
    )
    normed = (
        mid_stream
        * lax.rsqrt(jnp.mean(mid_stream * mid_stream, axis=-1, keepdims=True) + norm_eps)
        * norm_gain
    )
    rotated = rotate_rows(normed)
    expert_total = lax.axis_size(CHIPS)
    slot_total = slot_hot.shape[1]
    step = slot_total // CHUNKS
    hot_rows = slot_hot.astype(jnp.bfloat16).T
    gate_high = lax.reduce_precision(slot_gate, 8, 7)
    gate_parts = jnp.concatenate([gate_high, slot_gate - gate_high], axis=0).astype(jnp.bfloat16)
    gate_turned = jnp.swapaxes(gate_weight, 1, 2)
    up_turned = jnp.swapaxes(up_weight, 1, 2)
    swap = [(0, 1), (1, 0)]

    def exchange(blocks):
        return lax.all_to_all(blocks, CHIPS, split_axis=0, concat_axis=0, tiled=True)

    expert_sum = 0.0
    for chunk in range(CHUNKS):
        part = slice(chunk * step, (chunk + 1) * step)
        outgoing = pack_rows(hot_rows[part], rotated).reshape(expert_total, -1, feature_count)
        arrived = exchange(outgoing)
        theirs = lax.ppermute(arrived, "core", swap)
        made_mine, made_theirs = expert_half(
            arrived.reshape(step, feature_count),
            theirs.reshape(step, feature_count),
            gate_turned,
            up_turned,
            down_weight,
        )
        other_half = lax.ppermute(made_theirs.reshape(arrived.shape), "core", swap)
        summed = made_mine.reshape(arrived.shape).astype(jnp.float32) + other_half.astype(
            jnp.float32
        )
        returned = exchange(summed.astype(jnp.bfloat16)).reshape(step, feature_count)
        weighted = jnp.dot(gate_parts[:, part], returned, preferred_element_type=jnp.float32)
        expert_sum = expert_sum + weighted[:row_count] + weighted[row_count:]
    return (mid_stream + expert_sum).astype(jnp.bfloat16)


def route_tables(expert_ids, gate_values, expert_total):
    row_count, top_count = expert_ids.shape
    capacity = max(2, 2 * row_count * top_count // expert_total)
    experts = jnp.arange(expert_total, dtype=jnp.int32)
    named = expert_ids[:, :, None] == experts[None, None, :]
    chosen = jnp.any(named, axis=1).astype(jnp.float32)
    row_axis = jnp.arange(row_count, dtype=jnp.int32)
    earlier = (row_axis[:, None] > row_axis[None, :]).astype(jnp.float32)
    rank = jnp.dot(earlier, chosen, preferred_element_type=jnp.float32)
    route_rank = jnp.sum(jnp.where(named, rank[:, None, :], 0.0), axis=2).astype(jnp.int32)
    depth = capacity // CHUNKS
    slot = (
        route_rank // depth * (expert_total * depth) + expert_ids * depth + route_rank % depth
    )
    slots = jnp.arange(expert_total * capacity, dtype=jnp.int32)
    slot_hot = jnp.zeros((row_count, slots.shape[0]), jnp.float32)
    slot_gate = slot_hot
    for k in range(top_count):
        here = slot[:, k : k + 1] == slots[None, :]
        slot_hot = jnp.where(here, 1.0, slot_hot)
        slot_gate = jnp.where(here, gate_values[:, k : k + 1], slot_gate)
    return slot_hot, slot_gate


def solution(mesh):
    ctx_size, exp_size = mesh.devices.shape
    mesh = Mesh(mesh.devices.reshape(ctx_size, exp_size // 2, 2), AXES)
    in_specs = (
        P(AXES, None),
        P(AXES, None),
        P(AXES, None),
        P(AXES, None),
        P(),
        P(),
        P(),
        P(AXES, None, None),
        P(AXES, None, None),
        P(AXES, None, None),
        P(AXES, None),
        P(AXES, None),
    )
    out_specs = P(AXES, None)
    return jax.shard_map(local, mesh=mesh, in_specs=in_specs, out_specs=out_specs, check_vma=False)
```
